32 devices in a mesh: block: 4 (over y, x), tok: 8 (over z, core).
Axes of the slice: x: 2, y: 2, z: 4, core: 2. Of those that a mesh axis runs over, the one named last changes fastest.
Arguments:
- keys: bfloat16 [4, 2, 2048, 1280], P('block', None, 'tok'), may hold values from -6 to 6
- values: bfloat16 [4, 2, 2048, 1280], P('block', None, 'tok'), may hold values from -6 to 6
- queries: bfloat16 [4, 2, 2048, 1280], P('block', None, 'tok'), may hold values from -6 to 6
- rates: bfloat16 [4, 2, 2048, 20], P('block', None, 'tok'), may hold values from 0.00049972534 to 0.0049743652
- counts: int32 [4, 2, 8, 20], P('block', None, 'tok'), may hold values from 1 to 256
- stagger: int32 [20], replicated, may hold values from 0 to 255
- gate_in: bfloat16 [4, 20, 64, 512], P('block', None, None, 'tok'), may hold values from -0.75 to 0.75
- up_in: bfloat16 [4, 20, 64, 512], P('block', None, None, 'tok'), may hold values from -0.75 to 0.75
- down_in: bfloat16 [4, 20, 64, 512], P('block', None, None, 'tok'), may hold values from -0.25 to 0.25
- entry_gate: bfloat16 [20, 64, 512], replicated, may hold values from -0.75 to 0.75
- entry_up: bfloat16 [20, 64, 512], replicated, may hold values from -0.75 to 0.75
- entry_down: bfloat16 [20, 64, 512], replicated, may hold values from -0.25 to 0.25
Outputs:
- answers: bfloat16 [4, 2, 2048, 1280], P('block', None, 'tok')
- gate_out: bfloat16 [4, 20, 64, 512], P('block', None, None, 'tok')
- up_out: bfloat16 [4, 20, 64, 512], P('block', None, None, 'tok')
- down_out: bfloat16 [4, 20, 64, 512], P('block', None, None, 'tok')
The draws below stay inside these ranges and needn't reach their ends.
All inputs are finite; a program needn't handle non-finite values.
Results may differ from the reference program's by a relative error of at most 0.022.
Values may be sent and summed in bfloat16 or wider, within the bound.
A program may use at most 320 MiB of HBM per device.

```python
import math
import jax
import jax.numpy as jnp
from jax import lax

HEADS = 20
DH = 64
FH = 512
ROWS = 256
TICKS = 2
NCHUNK = 4
TOKS = 2048
N_TOK = 8


def touch_ends(values, own_key, low, high):
    dims = values.shape
    spot = [jax.random.randint(jax.random.fold_in(own_key, axis), (), 0, dims[axis]) for axis in range(len(dims))]
    values = values.at[tuple(spot)].set(low)
    longest = dims.index(max(dims))
    spot[longest] = (spot[longest] + 1) % dims[longest]
    return values.at[tuple(spot)].set(high)


def steps_of(key, extent, shards, least, top_value):
    loudness, own = 1.0, jax.random.fold_in(key, 6)
    for dim, blocks in shards:
        draws = jnp.exp(jax.random.uniform(jax.random.fold_in(own, dim), (blocks,), jnp.float32, least / len(shards), top_value / len(shards)))
        loudness = loudness * jnp.repeat(draws, extent[dim] // blocks).reshape([-1 if axis == dim else 1 for axis in range(len(extent))])
    return loudness


def centred(own_key, extent, scale, most, shards=(), held_as=jnp.bfloat16):
    values = scale * jax.random.normal(own_key, extent, jnp.float32)
    if shards:
        values = values * steps_of(own_key, extent, shards, -0.22, 0.18)
    return jnp.clip(values, -most, most).astype(held_as)


def setup_inputs(seed: int = 0) -> dict:
    key_of = jax.random.split(jax.random.key(seed), 13)
    return {
        "keys": centred(key_of[0], (NCHUNK, TICKS, TOKS, HEADS * DH), 1.0, 6.0, ((0, 4), (2, 8))),
        "values": centred(key_of[1], (NCHUNK, TICKS, TOKS, HEADS * DH), 1.0, 6.0, ((0, 4), (2, 8))),
        "queries": centred(key_of[2], (NCHUNK, TICKS, TOKS, HEADS * DH), 1.0, 6.0, ((0, 4), (2, 8))),
        "rates": jnp.clip(jnp.exp(math.log(0.0049743652) - 2.2979944 * jax.random.uniform(key_of[3], (NCHUNK, TICKS, TOKS, HEADS), jnp.float32) ** steps_of(key_of[3], (NCHUNK, TICKS, TOKS, HEADS), ((0, 4), (2, 8)), -0.2, 0.2)), 0.00049972534, 0.0049743652).astype(jnp.bfloat16),
        "counts": touch_ends(jax.random.randint(key_of[4], (NCHUNK, TICKS, N_TOK, HEADS), 1, ROWS + 1), jax.random.fold_in(key_of[4], 1), 1, ROWS).astype(jnp.int32),
        "stagger": touch_ends(jax.random.randint(key_of[5], (HEADS,), 0, ROWS), jax.random.fold_in(key_of[5], 1), 0, ROWS - 1).astype(jnp.int32),
        "gate_in": centred(key_of[6], (NCHUNK, HEADS, DH, FH), DH ** -0.5, 0.75, ((0, 4), (3, 8))),
        "up_in": centred(key_of[7], (NCHUNK, HEADS, DH, FH), DH ** -0.5, 0.75, ((0, 4), (3, 8))),
        "down_in": centred(key_of[8], (NCHUNK, HEADS, DH, FH), FH ** -0.5, 0.25, ((0, 4), (3, 8))),
        "entry_gate": centred(key_of[9], (HEADS, DH, FH), DH ** -0.5, 0.75),
        "entry_up": centred(key_of[10], (HEADS, DH, FH), DH ** -0.5, 0.75),
        "entry_down": centred(key_of[11], (HEADS, DH, FH), FH ** -0.5, 0.25),
    }


EPS = 1e-06

def gradients(keys, values, scale, weights):
    gate_w, up_w, down_w = weights
    rows = keys.shape[0]
    heads = gate_w.shape[0]
    size = gate_w.shape[1]
    kk = keys.reshape(rows, heads, size).astype(jnp.float32)
    vv = values.reshape(rows, heads, size).astype(jnp.float32)
    pre_gate = jnp.einsum('rhd,hdf->rhf', kk, gate_w.astype(jnp.float32))
    pre_up = jnp.einsum('rhd,hdf->rhf', kk, up_w.astype(jnp.float32))
    back = jnp.einsum('rhd,hdf->rhf', vv, down_w.astype(jnp.float32))
    weight = scale.astype(jnp.float32)[:, :, None]
    sig = jax.nn.sigmoid(pre_gate)
    act = pre_gate * sig
    hidden = (weight * act * pre_up).astype(jnp.bfloat16)
    d_gate = (weight * back * pre_up * sig * (1.0 + pre_gate * (1.0 - sig))).astype(jnp.bfloat16)
    d_up = (weight * back * act).astype(jnp.bfloat16)
    step_gate = jnp.einsum('rhd,rhf->hdf', kk, d_gate.astype(jnp.float32))
    step_up = jnp.einsum('rhd,rhf->hdf', kk, d_up.astype(jnp.float32))
    step_down = jnp.einsum('rhd,rhf->hdf', vv, hidden.astype(jnp.float32))
    return (step_gate, step_up, step_down)

def renew(weights, steps):
    result = []
    for weight, step in zip(weights, steps):
        base = weight.astype(jnp.float32)
        moved = base + step
        before = jnp.sqrt(lax.optimization_barrier(jnp.sum(base * base, axis=1, keepdims=True)) + EPS)
        after = jnp.sqrt(lax.optimization_barrier(jnp.sum(moved * moved, axis=1, keepdims=True)) + EPS)
        result.append((moved * (before / after)).astype(jnp.bfloat16))
    return tuple(result)

def respond(queries, weights):
    gate_w, up_w, down_w = weights
    rows = queries.shape[0]
    heads = gate_w.shape[0]
    size = gate_w.shape[1]
    qq = queries.reshape(rows, heads, size).astype(jnp.float32)
    pre_gate = jnp.einsum('rhd,hdf->rhf', qq, gate_w.astype(jnp.float32))
    pre_up = jnp.einsum('rhd,hdf->rhf', qq, up_w.astype(jnp.float32))
    hidden = (jax.nn.silu(pre_gate) * pre_up).astype(jnp.bfloat16)
    output = jnp.einsum('rhf,hdf->rhd', hidden.astype(jnp.float32), down_w.astype(jnp.float32))
    return output.reshape(rows, heads * size)

def reference(keys, values, queries, rates, counts, stagger, gate_in, up_in, down_in, entry_gate, entry_up, entry_down):
    index = jnp.arange(TOKS, dtype=jnp.int32)
    shard = index // ROWS
    offset = index % ROWS
    inside = jnp.mod(offset[:, None] - stagger[None, :].astype(jnp.int32), ROWS)

    def one_tick(items):
        kk, vv, qq, rr, cc, g_w, u_w, d_w = items
        limit = cc[shard, :]
        scale = jnp.where(inside < limit, rr, jnp.zeros_like(rr))
        weights = (g_w, u_w, d_w)
        steps = gradients(kk, vv, scale, weights)
        renewed = renew(weights, steps)
        return (respond(qq, renewed).astype(jnp.bfloat16), renewed)
    first, mid = lax.map(one_tick, (keys[:, 0], values[:, 0], queries[:, 0], rates[:, 0], counts[:, 0], gate_in, up_in, down_in))
    entries = (entry_gate, entry_up, entry_down)
    carried = tuple((jnp.concatenate([e[None], m[:-1]], axis=0) for e, m in zip(entries, mid)))
    second, final = lax.map(one_tick, (keys[:, 1], values[:, 1], queries[:, 1], rates[:, 1], counts[:, 1], carried[0], carried[1], carried[2]))
    answers = jnp.stack([first, second], axis=1)
    return (answers, final[0], final[1], final[2])
```

```python
import math

import jax
import jax.numpy as jnp
from jax import lax
from jax.sharding import PartitionSpec as P

EPS = 1e-06


def row_scale(rates, counts, stagger):
    rows = rates.shape[1]
    offset = jnp.arange(rows, dtype=jnp.int32)[None, :, None]
    inside = jnp.mod(offset - stagger[None, None, :], rows)
    return jnp.where(inside < counts, rates, jnp.zeros_like(rates))


def gradients(kk, vv, scale, weights):
    gate_w, up_w, down_w = weights
    f32 = jnp.float32
    pre_gate = jnp.einsum("hdf,hdt->hft", gate_w, kk, preferred_element_type=f32)
    pre_up = jnp.einsum("hdf,hdt->hft", up_w, kk, preferred_element_type=f32)
    back = jnp.einsum("hdf,hdt->hft", down_w, vv, preferred_element_type=f32)
    weight = scale.astype(f32)[:, None, :]
    sig = jax.nn.sigmoid(pre_gate)
    act = pre_gate * sig
    hidden = (weight * act * pre_up).astype(jnp.bfloat16)
    d_gate = (weight * back * pre_up * sig * (1.0 + pre_gate * (1.0 - sig))).astype(jnp.bfloat16)
    d_up = (weight * back * act).astype(jnp.bfloat16)
    return (
        jnp.einsum("hdt,hft->hdf", kk, d_gate, preferred_element_type=f32),
        jnp.einsum("hdt,hft->hdf", kk, d_up, preferred_element_type=f32),
        jnp.einsum("hdt,hft->hdf", vv, hidden, preferred_element_type=f32),
    )


def renew(weights, steps):
    result = []
    for weight, step in zip(weights, steps):
        base = weight.astype(jnp.float32)
        moved = base + step
        before = jnp.sqrt(jnp.sum(base * base, axis=1, keepdims=True) + EPS)
        after = jnp.sqrt(jnp.sum(moved * moved, axis=1, keepdims=True) + EPS)
        result.append((moved * (before / after)).astype(jnp.bfloat16))
    return jnp.stack(result)


def respond(qq, weights):
    gate_w, up_w, down_w = weights
    f32 = jnp.float32
    pre_gate = jnp.einsum("hdf,hdt->hft", gate_w, qq, preferred_element_type=f32)
    pre_up = jnp.einsum("hdf,hdt->hft", up_w, qq, preferred_element_type=f32)
    hidden = (jax.nn.silu(pre_gate) * pre_up).astype(jnp.bfloat16)
    return jnp.einsum("hdf,hft->hdt", down_w, hidden, preferred_element_type=f32).astype(jnp.bfloat16)


def shards(keys, values, queries, rates, counts, stagger, gate_in, up_in, down_in, entry_gate, entry_up, entry_down):
    ticks, rows = keys.shape[1:3]
    heads, size, width = gate_in.shape[1:]
    count = lax.axis_size("tok")
    blocks = lax.axis_size("block")
    groups = math.gcd(heads, count)
    members = count // groups
    own = heads // groups
    me = lax.axis_index("tok")
    group, member = me // members, me % members
    across = [[z * members + c for z in range(groups)] for c in range(members)]
    within = [[z * members + c for c in range(members)] for z in range(groups)]

    def exchange(x):
        return lax.all_to_all(x, "tok", 0, 0, axis_index_groups=across)

    def gathered(x):
        return lax.all_gather(x, "tok", axis=0, axis_index_groups=within)

    def by_group(x):
        return x.reshape(rows, groups, own * size).transpose(1, 2, 0)

    scale = row_scale(rates[0], counts[0], stagger)
    pack, asked = [], []
    for tick in range(ticks):
        k, v, q = (by_group(x[0, tick]) for x in (keys, values, queries))
        s = scale[tick].reshape(rows, groups, own).transpose(1, 2, 0)
        pack.append(jnp.concatenate([k, v, s], axis=1))
        asked.append(q)
    w = jnp.stack([gate_in[0], up_in[0], down_in[0]])
    w = w.reshape(3, groups, own, size, width).transpose(1, 0, 2, 3, 4)
    w = exchange(w).transpose(1, 2, 3, 0, 4).reshape(3, own, size, groups * width)
    entry = jnp.stack([entry_gate, entry_up, entry_down]).reshape(3, heads, size, groups, members, width)
    entry = lax.dynamic_slice_in_dim(entry, group * own, own, 1)
    entry = lax.dynamic_index_in_dim(entry, member, 4, keepdims=False).reshape(w.shape)
    out = []
    edge = own * size
    for tick in range(ticks):
        got = gathered(exchange(pack[tick]))
        got = got.transpose(2, 0, 1, 3).reshape(got.shape[2], -1)
        kk = got[:edge].reshape(own, size, -1)
        vv = got[edge : 2 * edge].reshape(own, size, -1)
        new = renew(w, gradients(kk, vv, got[2 * edge :], w))
        qq = exchange(asked[tick]).reshape(groups, own, size, rows).transpose(1, 2, 0, 3)
        qq = qq.reshape(own, size, groups * rows)
        full = gathered(new).transpose(1, 2, 3, 0, 4).reshape(3, own, size, -1)
        ans = respond(qq, full).reshape(own * size, groups, rows).transpose(1, 0, 2)
        out.append(exchange(ans).reshape(heads * size, rows).T)
        w = new
        if tick + 1 < ticks:
            sent = lax.ppermute(new, "block", [(i, i + 1) for i in range(blocks - 1)])
            w = jnp.where(lax.axis_index("block") == 0, entry, sent)
    w = w.reshape(3, own, size, groups, width).transpose(3, 0, 1, 2, 4)
    w = exchange(w).transpose(1, 0, 2, 3, 4).reshape(3, 1, heads, size, width)
    return (jnp.stack(out)[None], w[0], w[1], w[2])


def solution(mesh):
    tokens = P("block", None, "tok", None)
    hidden = P("block", None, None, "tok")
    return jax.shard_map(
        shards,
        mesh=mesh,
        in_specs=(tokens,) * 5 + (P(),) + (hidden,) * 3 + (P(),) * 3,
        out_specs=(tokens, hidden, hidden, hidden),
        check_vma=False,
    )
```

```python
import functools
import math

import jax
import jax.numpy as jnp
from jax import lax
from jax.experimental import pallas as pl
from jax.experimental.pallas import tpu as pltpu
from jax.sharding import PartitionSpec as P

EPS = 1e-06
F32 = jnp.float32
BF16 = jnp.bfloat16
MESH = pl.DeviceIdType.MESH


def row_scale(rates, counts, stagger):
    rows = rates.shape[1]
    offset = jnp.arange(rows, dtype=jnp.int32)[None, :, None]
    inside = jnp.mod(offset - stagger[None, None, :], rows)
    return jnp.where(inside < counts, rates, jnp.zeros_like(rates))


def sigmoid(x):
    return 0.5 * jnp.tanh(0.5 * x) + 0.5


def nn(a, b):
    return lax.dot_general(a, b, (((1,), (0,)), ((), ())), preferred_element_type=F32)


def nt(a, b):
    return lax.dot_general(a, b, (((1,), (1,)), ((), ())), preferred_element_type=F32)


def turned(x):
    return x.astype(F32).T.astype(BF16)


def kernel(
    groups, members, own, size, blocks,
    pack_ref, ask_ref, w_ref, entry_ref, ans_ref, wout_ref,
    kv, qs, full, carry, reply, acc, gut, wt, gut_all,
    kv_send, kv_recv, relay_send, relay_recv, q_send, q_recv,
    w_send, w_recv, carry_sem, a_send, a_recv, local,
):
    ticks = pack_ref.shape[0]
    edge = own * size
    hid = w_ref.shape[3]
    block = lax.axis_index("block")
    me = lax.axis_index("tok")
    z = me // members
    c = lax.rem(me, members)

    def behind(i):
        return lax.rem(z - i + groups, groups)

    def ahead(i):
        return lax.rem(z + i, groups)

    def mate(j):
        return lax.rem(c + j, members)

    def mate_back(j):
        return lax.rem(c - j + members, members)

    def at(zz, cc):
        return (block, zz * members + cc)

    def remote(src, dst, send, recv, device):
        return pltpu.make_async_remote_copy(
            src_ref=src, dst_ref=dst, send_sem=send, recv_sem=recv,
            device_id=device, device_id_type=MESH,
        )

    barrier = pltpu.get_barrier_semaphore()
    for i in range(1, groups):
        pl.semaphore_signal(barrier, inc=1, device_id=at(ahead(i), c), device_id_type=MESH)
    for j in range(1, members):
        pl.semaphore_signal(barrier, inc=1, device_id=at(z, mate(j)), device_id_type=MESH)

    @pl.when(block > 0)
    def _():
        pl.semaphore_signal(barrier, inc=1, device_id=(block - 1, me), device_id_type=MESH)

    @pl.when(block < blocks - 1)
    def _():
        pl.semaphore_signal(barrier, inc=1, device_id=(block + 1, me), device_id_type=MESH)

    near = jnp.where(block > 0, 1, 0) + jnp.where(block < blocks - 1, 1, 0)
    pl.semaphore_wait(barrier, groups - 1 + members - 1 + near)

    def kv_out(t, i):
        return remote(pack_ref.at[t, ahead(i)], kv.at[t, c, z], kv_send.at[t, i], kv_recv.at[t, i], at(ahead(i), c))

    def q_out(t, i):
        return remote(ask_ref.at[t, ahead(i)], qs.at[t, z], q_send.at[t, i], q_recv.at[t, i], at(ahead(i), c))

    def relay(t, j, i):
        part = kv.at[t, c, behind(i)]
        return remote(part, part, relay_send.at[t, j, i], relay_recv.at[t, j, i], at(z, mate(j)))

    def w_out(t, j):
        part = full.at[t, c]
        return remote(part, part, w_send.at[t, j], w_recv.at[t, j], at(z, mate(j)))

    def a_out(t, i):
        return remote(reply.at[t, behind(i)], ans_ref.at[t, z], a_send.at[t, i], a_recv.at[t, i], at(behind(i), c))

    def pass_on():
        return remote(full.at[0, c], carry, carry_sem.at[0], carry_sem.at[1], (lax.rem(block + 1, blocks), me))

    def kv_own(t):
        return pltpu.make_async_copy(pack_ref.at[t, z], kv.at[t, c, z], local.at[0, t])

    def q_own(t):
        return pltpu.make_async_copy(ask_ref.at[t, z], qs.at[t, z], local.at[1, t])

    def a_own(t):
        return pltpu.make_async_copy(reply.at[t, z], ans_ref.at[t, z], local.at[2, t])

    for i in range(1, groups):
        kv_out(0, i).start()
    for t in range(ticks):
        kv_own(t).start()
        q_own(t).start()

    for t in range(ticks):
        weights = w_ref if t == 0 else carry
        if t > 0:

            @pl.when(block == 0)
            def _():
                carry[...] = entry_ref[...]

            @pl.when(block > 0)
            def _():
                pass_on().wait_recv()

        for h in range(own):
            gut[h, :hid, :] = turned(weights[0, h])
            gut[h, hid:, :] = turned(weights[1, h])
            wt[h] = turned(weights[2, h])
        acc[...] = jnp.zeros_like(acc)
        kv_own(t).wait()

        def chunk(n, carried, t=t):
            j, i = n // groups, lax.rem(n, groups)

            @pl.when((j == 0) & (i > 0))
            def _():
                kv_out(t, i).wait_recv()

            @pl.when(j == 0)
            def _():
                for jj in range(1, members):
                    relay(t, jj, i).start()

            @pl.when(j > 0)
            def _():
                relay(t, j, i).wait_recv()

            part = kv.at[t, mate_back(j), behind(i)]
            scale = part[2 * edge :, :].astype(F32)
            for h in range(own):
                k = part[h * size : (h + 1) * size, :]
                v = part[edge + h * size : edge + (h + 1) * size, :]
                pre = nn(gut[h], k)
                back = nn(wt[h], v)
                gate, up = pre[:hid], pre[hid:]
                weight = scale[h : h + 1]
                sig = sigmoid(gate)
                act = gate * sig
                wb = weight * back
                hidden = (weight * act * up).astype(BF16)
                d_gate = (wb * up * (sig + act * (1.0 - sig))).astype(BF16)
                d_up = (wb * act).astype(BF16)
                acc[0, h] += nt(k, d_gate)
                acc[1, h] += nt(k, d_up)
                acc[2, h] += nt(v, hidden)
            return carried

        lax.fori_loop(0, groups, chunk, 0)
        if t == 0:
            for i in range(1, groups):
                q_out(0, i).start()
            for u in range(1, ticks):
                for i in range(1, groups):
                    kv_out(u, i).start()
                for i in range(1, groups):
                    q_out(u, i).start()
        lax.fori_loop(groups, groups * members, chunk, 0)

        for h in range(own):
            for p in range(3):
                base = weights[p, h].astype(F32)
                moved = base + acc[p, h]
                before = jnp.sum(base * base, axis=0, keepdims=True) + EPS
                after = jnp.sum(moved * moved, axis=0, keepdims=True) + EPS
                full[t, c, p, h] = (moved * (jnp.sqrt(before) / jnp.sqrt(after))).astype(BF16)
        for j in range(1, members):
            w_out(t, j).start()
        if t + 1 < ticks:

            @pl.when(block < blocks - 1)
            def _():
                pass_on().start()

        else:
            wout_ref[...] = full[t, c]
        for j in range(1, members):
            w_out(t, j).wait_recv()

        def prepare(s, carried, t=t):
            for h in range(own):
                gut_all[s, h, :hid, :] = turned(full[t, s, 0, h])
                gut_all[s, h, hid:, :] = turned(full[t, s, 1, h])
            return carried

        lax.fori_loop(0, members, prepare, 0)
        q_own(t).wait()

        def answer(n, carried, t=t):
            i = lax.rem(n + 1, groups)

            @pl.when(i > 0)
            def _():
                q_out(t, i).wait_recv()

            for h in range(own):
                q = qs[t, behind(i), h * size : (h + 1) * size, :]
                total = None
                for s in range(members):
                    pre = nn(gut_all[s, h], q)
                    gate, up = pre[:hid], pre[hid:]
                    hidden = (gate * sigmoid(gate) * up).astype(BF16)
                    term = nn(full[t, s, 2, h], hidden)
                    total = term if total is None else total + term
                reply[t, behind(i), h * size : (h + 1) * size, :] = total.astype(BF16)

            @pl.when(i > 0)
            def _():
                a_out(t, i).start()

            return carried

        lax.fori_loop(0, groups, answer, 0)
        a_own(t).start()

    for t in range(ticks):
        a_own(t).wait()
        for i in range(1, groups):
            a_out(t, i).wait()
            kv_out(t, i).wait_send()
            q_out(t, i).wait_send()
        for j in range(1, members):
            w_out(t, j).wait_send()
            for i in range(groups):
                relay(t, j, i).wait_send()

    @pl.when(block < blocks - 1)
    def _():
        pass_on().wait_send()


def shards(keys, values, queries, rates, counts, stagger, gate_in, up_in, down_in, entry_gate, entry_up, entry_down):
    ticks, rows = keys.shape[1:3]
    heads, size, width = gate_in.shape[1:]
    count = lax.axis_size("tok")
    blocks = lax.axis_size("block")
    groups = math.gcd(heads, count)
    members = count // groups
    own = heads // groups
    hid = groups * width
    edge = own * size
    room = -own % 16
    me = lax.axis_index("tok")
    group, member = me // members, me % members
    across = [[z * members + c for z in range(groups)] for c in range(members)]

    def exchange(x):
        return lax.all_to_all(x, "tok", 0, 0, axis_index_groups=across)

    def by_group(x):
        return x.reshape(ticks, rows, groups, -1).transpose(0, 2, 3, 1)

    scale = by_group(row_scale(rates[0], counts[0], stagger))
    scale = jnp.pad(scale, ((0, 0), (0, 0), (0, room), (0, 0)))
    pack = jnp.concatenate([by_group(keys[0]), by_group(values[0]), scale], axis=2)
    asked = by_group(queries[0])
    w = jnp.stack([gate_in[0], up_in[0], down_in[0]])
    w = w.reshape(3, groups, own, size, width).transpose(1, 0, 2, 3, 4)
    w = exchange(w).transpose(1, 2, 3, 0, 4).reshape(3, own, size, hid)
    entry = jnp.stack([entry_gate, entry_up, entry_down]).reshape(3, heads, size, groups, members, width)
    entry = lax.dynamic_slice_in_dim(entry, group * own, own, 1)
    entry = lax.dynamic_index_in_dim(entry, member, 4, keepdims=False).reshape(w.shape)

    dma = pltpu.SemaphoreType.DMA
    vmem = pl.BlockSpec(memory_space=pltpu.VMEM)
    answers, new = pl.pallas_call(
        functools.partial(kernel, groups, members, own, size, blocks),
        out_shape=(
            jax.ShapeDtypeStruct((ticks, groups, edge, rows), BF16),
            jax.ShapeDtypeStruct(w.shape, BF16),
        ),
        in_specs=[vmem] * 4,
        out_specs=(pl.BlockSpec(memory_space=pl.ANY), vmem),
        scratch_shapes=[
            pltpu.VMEM((ticks, members, groups, pack.shape[2], rows), BF16),
            pltpu.VMEM((ticks, groups, edge, rows), BF16),
            pltpu.VMEM((ticks, members, *w.shape), BF16),
            pltpu.VMEM(w.shape, BF16),
            pltpu.VMEM((ticks, groups, edge, rows), BF16),
            pltpu.VMEM(w.shape, F32),
            pltpu.VMEM((own, 2 * hid, size), BF16),
            pltpu.VMEM((own, hid, size), BF16),
            pltpu.VMEM((members, own, 2 * hid, size), BF16),
            dma((ticks, groups)), dma((ticks, groups)),
            dma((ticks, members, groups)), dma((ticks, members, groups)),
            dma((ticks, groups)), dma((ticks, groups)),
            dma((ticks, members)), dma((ticks, members)),
            dma((2,)),
            dma((ticks, groups)), dma((ticks, groups)),
            dma((3, ticks)),
        ],
        compiler_params=pltpu.CompilerParams(collective_id=0, has_side_effects=True),
        name="ttt",
    )(pack, asked, w, entry)
    answers = answers.transpose(0, 3, 1, 2).reshape(1, ticks, rows, heads * size)
    new = new.reshape(3, own, size, groups, width).transpose(3, 0, 1, 2, 4)
    new = exchange(new).transpose(1, 0, 2, 3, 4).reshape(3, 1, heads, size, width)
    return (answers, new[0], new[1], new[2])


def solution(mesh):
    tokens = P("block", None, "tok", None)
    hidden = P("block", None, None, "tok")
    return jax.shard_map(
        shards,
        mesh=mesh,
        in_specs=(tokens,) * 5 + (P(),) + (hidden,) * 3 + (P(),) * 3,
        out_specs=(tokens, hidden, hidden, hidden),
        check_vma=False,
    )
```

```python
import functools
import math

import jax
import jax.numpy as jnp
from jax import lax
from jax.experimental import pallas as pl
from jax.experimental.pallas import tpu as pltpu
from jax.sharding import PartitionSpec as P

EPS = 1e-06
F32 = jnp.float32
BF16 = jnp.bfloat16
MESH = pl.DeviceIdType.MESH


def row_scale(rates, counts, stagger):
    rows = rates.shape[1]
    offset = jnp.arange(rows, dtype=jnp.int32)[None, :, None]
    inside = jnp.mod(offset - stagger[None, None, :], rows)
    return jnp.where(inside < counts, rates, jnp.zeros_like(rates))


def sigmoid(x):
    return 0.5 * jnp.tanh(0.5 * x) + 0.5


def nn(a, b):
    return lax.dot_general(a, b, (((1,), (0,)), ((), ())), preferred_element_type=F32)


def nt(a, b):
    return lax.dot_general(a, b, (((1,), (1,)), ((), ())), preferred_element_type=F32)


def turned(x):
    return x.astype(F32).T.astype(BF16)


def kernel(
    groups, members, own, size, blocks,
    pack_ref, ask_ref, pair_ref, down_ref, entry0, entry1, entry2, ans_ref, pair_out, down_out,
    kv, qs, first, pairs, downs, pair_back, down_back, entry, full, carry, reply, acc, gut, wt, gut_all,
    kv_send, kv_recv, relay_send, relay_recv, q_send, q_recv,
    g_send, g_recv, d_send, d_recv, gb_send, gb_recv, db_send, db_recv, entry_sem, w_send, w_recv, carry_sem, a_send, a_recv, local,
):
    ticks = pack_ref.shape[0]
    edge = own * size
    hid = first.shape[3]
    width = hid // groups
    block = lax.axis_index("block")
    me = lax.axis_index("tok")
    z = me // members
    c = lax.rem(me, members)

    def behind(i):
        return lax.rem(z - i + groups, groups)

    def ahead(i):
        return lax.rem(z + i, groups)

    def mate(j):
        return lax.rem(c + j, members)

    def mate_back(j):
        return lax.rem(c - j + members, members)

    def at(zz, cc):
        return (block, zz * members + cc)

    def remote(src, dst, send, recv, device):
        return pltpu.make_async_remote_copy(
            src_ref=src, dst_ref=dst, send_sem=send, recv_sem=recv,
            device_id=device, device_id_type=MESH,
        )

    barrier = pltpu.get_barrier_semaphore()
    for i in range(1, groups):
        pl.semaphore_signal(barrier, inc=1, device_id=at(ahead(i), c), device_id_type=MESH)
    for j in range(1, members):
        pl.semaphore_signal(barrier, inc=1, device_id=at(z, mate(j)), device_id_type=MESH)

    @pl.when(block > 0)
    def _():
        pl.semaphore_signal(barrier, inc=1, device_id=(block - 1, me), device_id_type=MESH)

    @pl.when(block < blocks - 1)
    def _():
        pl.semaphore_signal(barrier, inc=1, device_id=(block + 1, me), device_id_type=MESH)

    near = jnp.where(block > 0, 1, 0) + jnp.where(block < blocks - 1, 1, 0)
    pl.semaphore_wait(barrier, groups - 1 + members - 1 + near)

    def kv_out(t, i):
        return remote(pack_ref.at[t, ahead(i)], kv.at[t, c, z], kv_send.at[t, i], kv_recv.at[t, i], at(ahead(i), c))

    def q_out(t, i):
        return remote(ask_ref.at[t, ahead(i)], qs.at[t, z], q_send.at[t, i], q_recv.at[t, i], at(ahead(i), c))

    def relay(t, j, i):
        part = kv.at[t, c, behind(i)]
        return remote(part, part, relay_send.at[t, j, i], relay_recv.at[t, j, i], at(z, mate(j)))

    def w_out(t, j):
        part = full.at[t, c]
        return remote(part, part, w_send.at[t, j], w_recv.at[t, j], at(z, mate(j)))

    def a_out(t, i):
        return remote(reply.at[t, behind(i)], ans_ref.at[t, z], a_send.at[t, i], a_recv.at[t, i], at(behind(i), c))

    def pass_on():
        return remote(full.at[0, c], carry, carry_sem.at[0], carry_sem.at[1], (lax.rem(block + 1, blocks), me))

    def pair_put(i):
        return remote(pair_ref.at[ahead(i)], pairs.at[z], g_send.at[i], g_recv.at[i], at(ahead(i), c))

    def down_put(i):
        return remote(down_ref.at[ahead(i)], downs.at[z], d_send.at[i], d_recv.at[i], at(ahead(i), c))

    def pair_give(i):
        return remote(pair_back.at[ahead(i)], pair_out.at[z], gb_send.at[i], gb_recv.at[i], at(ahead(i), c))

    def down_give(i):
        return remote(down_back.at[ahead(i)], down_out.at[z], db_send.at[i], db_recv.at[i], at(ahead(i), c))

    def w_own():
        return (
            pltpu.make_async_copy(pair_ref.at[z], pairs.at[z], local.at[3, 0]),
            pltpu.make_async_copy(down_ref.at[z], downs.at[z], local.at[3, 1]),
        )

    def w_back():
        return (
            pltpu.make_async_copy(pair_back.at[z], pair_out.at[z], local.at[4, 0]),
            pltpu.make_async_copy(down_back.at[z], down_out.at[z], local.at[4, 1]),
        )

    def entry_own(p):
        whole = (entry0, entry1, entry2)[p]
        return pltpu.make_async_copy(whole.at[pl.ds(z * own, own)], entry.at[p], entry_sem.at[p])

    def kv_own(t):
        return pltpu.make_async_copy(pack_ref.at[t, z], kv.at[t, c, z], local.at[0, t])

    def q_own(t):
        return pltpu.make_async_copy(ask_ref.at[t, z], qs.at[t, z], local.at[1, t])

    def a_own(t):
        return pltpu.make_async_copy(reply.at[t, z], ans_ref.at[t, z], local.at[2, t])

    for i in range(1, groups):
        pair_put(i).start()
        down_put(i).start()
    for i in range(1, groups):
        kv_out(0, i).start()
    for copy in w_own():
        copy.start()
    for t in range(ticks):
        kv_own(t).start()
        q_own(t).start()
    for p in range(3):
        entry_own(p).start()
    for copy in w_own():
        copy.wait()
    for i in range(1, groups):
        pair_put(i).wait_recv()
        down_put(i).wait_recv()
    for h in range(own):
        for p, (held, low) in enumerate(((pairs, 0), (pairs, width), (downs, 0))):
            parts = [held[zz, h, :, low : low + width] for zz in range(groups)]
            first[p, h] = jnp.concatenate(parts, axis=1)

    for t in range(ticks):
        weights = first if t == 0 else carry
        if t > 0:

            for p in range(3):
                entry_own(p).wait()
            for s in range(members):

                @pl.when((block == 0) & (c == s))
                def _(s=s):
                    for p in range(3):
                        for h in range(own):
                            lows = [(zz * members + s) * width for zz in range(groups)]
                            parts = [entry[p, h, :, low : low + width] for low in lows]
                            carry[p, h] = jnp.concatenate(parts, axis=1)

            @pl.when(block > 0)
            def _():
                pass_on().wait_recv()

        for h in range(own):
            gut[h, :hid, :] = turned(weights[0, h])
            gut[h, hid:, :] = turned(weights[1, h])
            wt[h] = turned(weights[2, h])
        acc[...] = jnp.zeros_like(acc)
        kv_own(t).wait()

        def chunk(n, carried, t=t):
            j, i = n // groups, lax.rem(n, groups)

            @pl.when((j == 0) & (i > 0))
            def _():
                kv_out(t, i).wait_recv()

            @pl.when(j == 0)
            def _():
                for jj in range(1, members):
                    relay(t, jj, i).start()

            @pl.when(j > 0)
            def _():
                relay(t, j, i).wait_recv()

            part = kv.at[t, mate_back(j), behind(i)]
            scale = part[2 * edge :, :].astype(F32)
            for h in range(own):
                k = part[h * size : (h + 1) * size, :]
                v = part[edge + h * size : edge + (h + 1) * size, :]
                pre = nn(gut[h], k)
                back = nn(wt[h], v)
                gate, up = pre[:hid], pre[hid:]
                weight = scale[h : h + 1]
                sig = sigmoid(gate)
                act = gate * sig
                wb = weight * back
                hidden = (weight * act * up).astype(BF16)
                d_gate = (wb * up * (sig + act * (1.0 - sig))).astype(BF16)
                d_up = (wb * act).astype(BF16)
                acc[0, h] += nt(k, d_gate)
                acc[1, h] += nt(k, d_up)
                acc[2, h] += nt(v, hidden)
            return carried

        lax.fori_loop(0, groups, chunk, 0)
        if t == 0:
            for i in range(1, groups):
                q_out(0, i).start()
            for u in range(1, ticks):
                for i in range(1, groups):
                    kv_out(u, i).start()
                for i in range(1, groups):
                    q_out(u, i).start()
        lax.fori_loop(groups, groups * members, chunk, 0)

        for h in range(own):
            for p in range(3):
                base = weights[p, h].astype(F32)
                moved = base + acc[p, h]
                before = jnp.sum(base * base, axis=0, keepdims=True) + EPS
                after = jnp.sum(moved * moved, axis=0, keepdims=True) + EPS
                full[t, c, p, h] = (moved * (jnp.sqrt(before) / jnp.sqrt(after))).astype(BF16)
        for j in range(1, members):
            w_out(t, j).start()
        if t + 1 < ticks:

            @pl.when(block < blocks - 1)
            def _():
                pass_on().start()

        else:
            for zz in range(groups):
                lanes = slice(zz * width, (zz + 1) * width)
                for h in range(own):
                    pair_back[zz, h, :, :width] = full[t, c, 0, h, :, lanes]
                    pair_back[zz, h, :, width:] = full[t, c, 1, h, :, lanes]
                    down_back[zz, h] = full[t, c, 2, h, :, lanes]
            for i in range(1, groups):
                pair_give(i).start()
                down_give(i).start()
            for copy in w_back():
                copy.start()
        for j in range(1, members):
            w_out(t, j).wait_recv()

        def prepare(s, carried, t=t):
            for h in range(own):
                gut_all[s, h, :hid, :] = turned(full[t, s, 0, h])
                gut_all[s, h, hid:, :] = turned(full[t, s, 1, h])
            return carried

        lax.fori_loop(0, members, prepare, 0)
        q_own(t).wait()

        def answer(n, carried, t=t):
            i = lax.rem(n + 1, groups)

            @pl.when(i > 0)
            def _():
                q_out(t, i).wait_recv()

            for h in range(own):
                q = qs[t, behind(i), h * size : (h + 1) * size, :]
                total = None
                for s in range(members):
                    pre = nn(gut_all[s, h], q)
                    gate, up = pre[:hid], pre[hid:]
                    hidden = (gate * sigmoid(gate) * up).astype(BF16)
                    term = nn(full[t, s, 2, h], hidden)
                    total = term if total is None else total + term
                reply[t, behind(i), h * size : (h + 1) * size, :] = total.astype(BF16)

            @pl.when(i > 0)
            def _():
                a_out(t, i).start()

            return carried

        lax.fori_loop(0, groups, answer, 0)
        a_own(t).start()

    for t in range(ticks):
        a_own(t).wait()
        for i in range(1, groups):
            a_out(t, i).wait()
            kv_out(t, i).wait_send()
            q_out(t, i).wait_send()
        for j in range(1, members):
            w_out(t, j).wait_send()
            for i in range(groups):
                relay(t, j, i).wait_send()

    for i in range(1, groups):
        pair_put(i).wait_send()
        down_put(i).wait_send()
        pair_give(i).wait()
        down_give(i).wait()
    for copy in w_back():
        copy.wait()

    @pl.when(block < blocks - 1)
    def _():
        pass_on().wait_send()


def shards(keys, values, queries, rates, counts, stagger, gate_in, up_in, down_in, entry_gate, entry_up, entry_down):
    ticks, rows = keys.shape[1:3]
    heads, size, width = gate_in.shape[1:]
    count = lax.axis_size("tok")
    blocks = lax.axis_size("block")
    groups = math.gcd(heads, count)
    members = count // groups
    own = heads // groups
    hid = groups * width
    edge = own * size
    room = -own % 16
    def by_group(x):
        return x.reshape(ticks, rows, groups, -1).transpose(0, 2, 3, 1)

    scale = by_group(row_scale(rates[0], counts[0], stagger))
    scale = jnp.pad(scale, ((0, 0), (0, 0), (0, room), (0, 0)))
    pack = jnp.concatenate([by_group(keys[0]), by_group(values[0]), scale], axis=2)
    asked = by_group(queries[0])
    pair = jnp.concatenate([gate_in[0], up_in[0]], axis=2).reshape(groups, own, size, 2 * width)
    down = down_in[0].reshape(groups, own, size, width)
    shape = (3, own, size, hid)

    dma = pltpu.SemaphoreType.DMA
    vmem = pl.BlockSpec(memory_space=pltpu.VMEM)
    hbm = pl.BlockSpec(memory_space=pl.ANY)
    answers, pair, down = pl.pallas_call(
        functools.partial(kernel, groups, members, own, size, blocks),
        out_shape=(
            jax.ShapeDtypeStruct((ticks, groups, edge, rows), BF16),
            jax.ShapeDtypeStruct(pair.shape, BF16),
            jax.ShapeDtypeStruct(down.shape, BF16),
        ),
        in_specs=[vmem] * 4 + [hbm] * 3,
        out_specs=(hbm, hbm, hbm),
        scratch_shapes=[
            pltpu.VMEM((ticks, members, groups, pack.shape[2], rows), BF16),
            pltpu.VMEM((ticks, groups, edge, rows), BF16),
            pltpu.VMEM(shape, BF16),
            pltpu.VMEM(pair.shape, BF16),
            pltpu.VMEM(down.shape, BF16),
            pltpu.VMEM(pair.shape, BF16),
            pltpu.VMEM(down.shape, BF16),
            pltpu.VMEM((3, own, size, entry_gate.shape[2]), BF16),
            pltpu.VMEM((ticks, members, *shape), BF16),
            pltpu.VMEM(shape, BF16),
            pltpu.VMEM((ticks, groups, edge, rows), BF16),
            pltpu.VMEM(shape, F32),
            pltpu.VMEM((own, 2 * hid, size), BF16),
            pltpu.VMEM((own, hid, size), BF16),
            pltpu.VMEM((members, own, 2 * hid, size), BF16),
            dma((ticks, groups)), dma((ticks, groups)),
            dma((ticks, members, groups)), dma((ticks, members, groups)),
            dma((ticks, groups)), dma((ticks, groups)),
            *[dma((groups,)) for _ in range(8)],
            dma((3,)),
            dma((ticks, members)), dma((ticks, members)),
            dma((2,)),
            dma((ticks, groups)), dma((ticks, groups)),
            dma((5, max(2, ticks))),
        ],
        compiler_params=pltpu.CompilerParams(collective_id=0, has_side_effects=True),
        name="ttt",
    )(pack, asked, pair, down, entry_gate, entry_up, entry_down)
    answers = answers.transpose(0, 3, 1, 2).reshape(1, ticks, rows, heads * size)
    pair = pair.reshape(1, heads, size, 2 * width)
    return (answers, pair[..., :width], pair[..., width:], down.reshape(1, heads, size, width))


def solution(mesh):
    tokens = P("block", None, "tok", None)
    hidden = P("block", None, None, "tok")
    return jax.shard_map(
        shards,
        mesh=mesh,
        in_specs=(tokens,) * 5 + (P(),) + (hidden,) * 3 + (P(),) * 3,
        out_specs=(tokens, hidden, hidden, hidden),
        check_vma=False,
    )
```

```python
import functools
import math

import jax
import jax.numpy as jnp
from jax import lax
from jax.experimental import pallas as pl
from jax.experimental.pallas import tpu as pltpu
from jax.sharding import PartitionSpec as P

EPS = 1e-06
F32 = jnp.float32
BF16 = jnp.bfloat16
MESH = pl.DeviceIdType.MESH


def row_scale(rates, counts, stagger):
    rows = rates.shape[1]
    offset = jnp.arange(rows, dtype=jnp.int32)[None, :, None]
    inside = jnp.mod(offset - stagger[None, None, :], rows)
    return jnp.where(inside < counts, rates, jnp.zeros_like(rates))


def sigmoid(x):
    return 0.5 * jnp.tanh(0.5 * x) + 0.5


def nn(a, b):
    return lax.dot_general(a, b, (((1,), (0,)), ((), ())), preferred_element_type=F32)


def nt(a, b):
    return lax.dot_general(a, b, (((1,), (1,)), ((), ())), preferred_element_type=F32)


def turned(x):
    return x.astype(F32).T.astype(BF16)


def kernel(
    groups, members, own, size, blocks,
    pack_ref, ask_ref, pair_ref, entry0, entry1, entry2, ans_ref, pair_out,
    kv, qs, first, pairs, pair_back, entry, full, carry, reply, acc, gut, wt, gut_all,
    kv_send, kv_recv, relay_send, relay_recv, q_send, q_recv,
    g_send, g_recv, gb_send, gb_recv, entry_sem, w_send, w_recv, carry_sem, a_send, a_recv, local,
):
    ticks = pack_ref.shape[0]
    edge = own * size
    hid = first.shape[3]
    width = hid // groups
    half = pairs.shape[1]
    block = lax.axis_index("block")
    me = lax.axis_index("tok")
    z = me // members
    c = lax.rem(me, members)

    def behind(i):
        return lax.rem(z - i + groups, groups)

    def ahead(i):
        return lax.rem(z + i, groups)

    def mate(j):
        return lax.rem(c + j, members)

    def mate_back(j):
        return lax.rem(c - j + members, members)

    def at(zz, cc):
        return (block, zz * members + cc)

    def remote(src, dst, send, recv, device):
        return pltpu.make_async_remote_copy(
            src_ref=src, dst_ref=dst, send_sem=send, recv_sem=recv,
            device_id=device, device_id_type=MESH,
        )

    barrier = pltpu.get_barrier_semaphore()
    for i in range(1, groups):
        pl.semaphore_signal(barrier, inc=1, device_id=at(ahead(i), c), device_id_type=MESH)
    for j in range(1, members):
        pl.semaphore_signal(barrier, inc=1, device_id=at(z, mate(j)), device_id_type=MESH)

    @pl.when(block > 0)
    def _():
        pl.semaphore_signal(barrier, inc=1, device_id=(block - 1, me), device_id_type=MESH)

    @pl.when(block < blocks - 1)
    def _():
        pl.semaphore_signal(barrier, inc=1, device_id=(block + 1, me), device_id_type=MESH)

    near = jnp.where(block > 0, 1, 0) + jnp.where(block < blocks - 1, 1, 0)
    pl.semaphore_wait(barrier, groups - 1 + members - 1 + near)

    def kv_out(t, i):
        return remote(pack_ref.at[t, ahead(i)], kv.at[t, c, z], kv_send.at[t, i], kv_recv.at[t, i], at(ahead(i), c))

    def q_out(t, i):
        return remote(ask_ref.at[t, ahead(i)], qs.at[t, z], q_send.at[t, i], q_recv.at[t, i], at(ahead(i), c))

    def relay(t, j, i):
        part = kv.at[t, c, behind(i)]
        return remote(part, part, relay_send.at[t, j, i], relay_recv.at[t, j, i], at(z, mate(j)))

    def w_out(t, j):
        part = full.at[t, c]
        return remote(part, part, w_send.at[t, j], w_recv.at[t, j], at(z, mate(j)))

    def a_out(t, i):
        return remote(reply.at[t, behind(i)], ans_ref.at[t, z], a_send.at[t, i], a_recv.at[t, i], at(behind(i), c))

    def pass_on():
        return remote(full.at[0, c], carry, carry_sem.at[0], carry_sem.at[1], (lax.rem(block + 1, blocks), me))

    def pair_put(i):
        return remote(pair_ref.at[ahead(i)], pairs.at[z], g_send.at[i], g_recv.at[i], at(ahead(i), c))

    def pair_give(i):
        return remote(pair_back.at[ahead(i)], pair_out.at[z], gb_send.at[i], gb_recv.at[i], at(ahead(i), c))

    def w_own():
        return pltpu.make_async_copy(pair_ref.at[z], pairs.at[z], local.at[3, 0])

    def w_back():
        return pltpu.make_async_copy(pair_back.at[z], pair_out.at[z], local.at[4, 0])

    def entry_own(p):
        whole = (entry0, entry1, entry2)[p]
        return pltpu.make_async_copy(whole.at[pl.ds(z * own, own)], entry.at[p], entry_sem.at[p])

    def kv_own(t):
        return pltpu.make_async_copy(pack_ref.at[t, z], kv.at[t, c, z], local.at[0, t])

    def q_own(t):
        return pltpu.make_async_copy(ask_ref.at[t, z], qs.at[t, z], local.at[1, t])

    def a_own(t):
        return pltpu.make_async_copy(reply.at[t, z], ans_ref.at[t, z], local.at[2, t])

    for i in range(1, groups):
        pair_put(i).start()
    for i in range(1, groups):
        kv_out(0, i).start()
    w_own().start()
    for t in range(ticks):
        kv_own(t).start()
        q_own(t).start()
    for p in range(3):
        entry_own(p).start()
    w_own().wait()
    for i in range(1, groups):
        pair_put(i).wait_recv()
    for h in range(own):
        for p in range(3):
            spot, side = (p * own + h) % half, (p * own + h) // half * width
            parts = [pairs[zz, spot, :, side : side + width] for zz in range(groups)]
            first[p, h] = jnp.concatenate(parts, axis=1)

    for t in range(ticks):
        weights = first if t == 0 else carry
        if t > 0:

            for p in range(3):
                entry_own(p).wait()
            for s in range(members):

                @pl.when((block == 0) & (c == s))
                def _(s=s):
                    for p in range(3):
                        for h in range(own):
                            lows = [(zz * members + s) * width for zz in range(groups)]
                            parts = [entry[p, h, :, low : low + width] for low in lows]
                            carry[p, h] = jnp.concatenate(parts, axis=1)

            @pl.when(block > 0)
            def _():
                pass_on().wait_recv()

        for h in range(own):
            gut[h, :hid, :] = turned(weights[0, h])
            gut[h, hid:, :] = turned(weights[1, h])
            wt[h] = turned(weights[2, h])
        acc[...] = jnp.zeros_like(acc)
        kv_own(t).wait()

        def chunk(n, carried, t=t):
            j, i = n // groups, lax.rem(n, groups)

            @pl.when((j == 0) & (i > 0))
            def _():
                kv_out(t, i).wait_recv()

            @pl.when(j == 0)
            def _():
                for jj in range(1, members):
                    relay(t, jj, i).start()

            @pl.when(j > 0)
            def _():
                relay(t, j, i).wait_recv()

            part = kv.at[t, mate_back(j), behind(i)]
            scale = part[2 * edge :, :].astype(F32)
            for h in range(own):
                k = part[h * size : (h + 1) * size, :]
                v = part[edge + h * size : edge + (h + 1) * size, :]
                pre = nn(gut[h], k)
                back = nn(wt[h], v)
                gate, up = pre[:hid], pre[hid:]
                weight = scale[h : h + 1]
                sig = sigmoid(gate)
                act = gate * sig
                wb = weight * back
                hidden = (weight * act * up).astype(BF16)
                d_gate = (wb * up * (sig + act * (1.0 - sig))).astype(BF16)
                d_up = (wb * act).astype(BF16)
                acc[0, h] += nt(k, d_gate)
                acc[1, h] += nt(k, d_up)
                acc[2, h] += nt(v, hidden)
            return carried

        lax.fori_loop(0, groups, chunk, 0)
        if t == 0:
            for i in range(1, groups):
                q_out(0, i).start()
            for u in range(1, ticks):
                for i in range(1, groups):
                    kv_out(u, i).start()
                for i in range(1, groups):
                    q_out(u, i).start()
        lax.fori_loop(groups, groups * members, chunk, 0)

        for h in range(own):
            for p in range(3):
                base = weights[p, h].astype(F32)
                moved = base + acc[p, h]
                before = jnp.sum(base * base, axis=0, keepdims=True) + EPS
                after = jnp.sum(moved * moved, axis=0, keepdims=True) + EPS
                full[t, c, p, h] = (moved * (jnp.sqrt(before) / jnp.sqrt(after))).astype(BF16)
        for j in range(1, members):
            w_out(t, j).start()
        if t + 1 < ticks:

            @pl.when(block < blocks - 1)
            def _():
                pass_on().start()

        else:
            for zz in range(groups):
                lanes = slice(zz * width, (zz + 1) * width)
                for n in range(2 * half):
                    spot, side = n % half, n // half * width
                    if n < 3 * own:
                        piece = full[t, c, n // own, n % own, :, lanes]
                    else:
                        piece = jnp.zeros((size, width), BF16)
                    pair_back[zz, spot, :, side : side + width] = piece
            for i in range(1, groups):
                pair_give(i).start()
            w_back().start()
        for j in range(1, members):
            w_out(t, j).wait_recv()

        def prepare(s, carried, t=t):
            for h in range(own):
                gut_all[s, h, :hid, :] = turned(full[t, s, 0, h])
                gut_all[s, h, hid:, :] = turned(full[t, s, 1, h])
            return carried

        lax.fori_loop(0, members, prepare, 0)
        q_own(t).wait()

        def answer(n, carried, t=t):
            i = lax.rem(n + 1, groups)

            @pl.when(i > 0)
            def _():
                q_out(t, i).wait_recv()

            for h in range(own):
                q = qs[t, behind(i), h * size : (h + 1) * size, :]
                total = None
                for s in range(members):
                    pre = nn(gut_all[s, h], q)
                    gate, up = pre[:hid], pre[hid:]
                    hidden = (gate * sigmoid(gate) * up).astype(BF16)
                    term = nn(full[t, s, 2, h], hidden)
                    total = term if total is None else total + term
                reply[t, behind(i), h * size : (h + 1) * size, :] = total.astype(BF16)

            @pl.when(i > 0)
            def _():
                a_out(t, i).start()

            return carried

        lax.fori_loop(0, groups, answer, 0)
        a_own(t).start()

    for t in range(ticks):
        a_own(t).wait()
        for i in range(1, groups):
            a_out(t, i).wait()
            kv_out(t, i).wait_send()
            q_out(t, i).wait_send()
        for j in range(1, members):
            w_out(t, j).wait_send()
            for i in range(groups):
                relay(t, j, i).wait_send()

    for i in range(1, groups):
        pair_put(i).wait_send()
        pair_give(i).wait()
    w_back().wait()

    @pl.when(block < blocks - 1)
    def _():
        pass_on().wait_send()


def shards(keys, values, queries, rates, counts, stagger, gate_in, up_in, down_in, entry_gate, entry_up, entry_down):
    ticks, rows = keys.shape[1:3]
    heads, size, width = gate_in.shape[1:]
    count = lax.axis_size("tok")
    blocks = lax.axis_size("block")
    groups = math.gcd(heads, count)
    members = count // groups
    own = heads // groups
    hid = groups * width
    edge = own * size
    room = -own % 16
    def by_group(x):
        return x.reshape(ticks, rows, groups, -1).transpose(0, 2, 3, 1)

    scale = by_group(row_scale(rates[0], counts[0], stagger))
    scale = jnp.pad(scale, ((0, 0), (0, 0), (0, room), (0, 0)))
    pack = jnp.concatenate([by_group(keys[0]), by_group(values[0]), scale], axis=2)
    asked = by_group(queries[0])
    half = (3 * own + 1) // 2
    slots = jnp.stack([gate_in[0], up_in[0], down_in[0]]).reshape(3, groups, own, size, width)
    slots = slots.transpose(1, 0, 2, 3, 4).reshape(groups, 3 * own, size, width)
    slots = jnp.pad(slots, ((0, 0), (0, 2 * half - 3 * own), (0, 0), (0, 0)))
    pair = jnp.concatenate([slots[:, :half], slots[:, half:]], axis=3)
    shape = (3, own, size, hid)

    dma = pltpu.SemaphoreType.DMA
    vmem = pl.BlockSpec(memory_space=pltpu.VMEM)
    hbm = pl.BlockSpec(memory_space=pl.ANY)
    answers, pair = pl.pallas_call(
        functools.partial(kernel, groups, members, own, size, blocks),
        out_shape=(
            jax.ShapeDtypeStruct((ticks, groups, edge, rows), BF16),
            jax.ShapeDtypeStruct(pair.shape, BF16),
        ),
        in_specs=[vmem] * 3 + [hbm] * 3,
        out_specs=(hbm, hbm),
        scratch_shapes=[
            pltpu.VMEM((ticks, members, groups, pack.shape[2], rows), BF16),
            pltpu.VMEM((ticks, groups, edge, rows), BF16),
            pltpu.VMEM(shape, BF16),
            pltpu.VMEM(pair.shape, BF16),
            pltpu.VMEM(pair.shape, BF16),
            pltpu.VMEM((3, own, size, entry_gate.shape[2]), BF16),
            pltpu.VMEM((ticks, members, *shape), BF16),
            pltpu.VMEM(shape, BF16),
            pltpu.VMEM((ticks, groups, edge, rows), BF16),
            pltpu.VMEM(shape, F32),
            pltpu.VMEM((own, 2 * hid, size), BF16),
            pltpu.VMEM((own, hid, size), BF16),
            pltpu.VMEM((members, own, 2 * hid, size), BF16),
            dma((ticks, groups)), dma((ticks, groups)),
            dma((ticks, members, groups)), dma((ticks, members, groups)),
            dma((ticks, groups)), dma((ticks, groups)),
            *[dma((groups,)) for _ in range(4)],
            dma((3,)),
            dma((ticks, members)), dma((ticks, members)),
            dma((2,)),
            dma((ticks, groups)), dma((ticks, groups)),
            dma((5, max(2, ticks))),
        ],
        compiler_params=pltpu.CompilerParams(collective_id=0, has_side_effects=True),
        name="ttt",
    )(pack, asked, pair, entry_gate, entry_up, entry_down)
    answers = answers.transpose(0, 3, 1, 2).reshape(1, ticks, rows, heads * size)
    slots = jnp.concatenate([pair[..., :width], pair[..., width:]], axis=1)[:, : 3 * own]
    new = slots.reshape(groups, 3, own, size, width)
    return (answers, *(new[:, p].reshape(1, heads, size, width) for p in range(3)))


def solution(mesh):
    tokens = P("block", None, "tok", None)
    hidden = P("block", None, None, "tok")
    return jax.shard_map(
        shards,
        mesh=mesh,
        in_specs=(tokens,) * 5 + (P(),) + (hidden,) * 3 + (P(),) * 3,
        out_specs=(tokens, hidden, hidden, hidden),
        check_vma=False,
    )
```
